32 devices in a mesh: dp: 4 (over y, core), expert: 4 (over z), tensor: 2 (over x).
Axes of the slice: x: 2, y: 2, z: 4, core: 2. Of those that a mesh axis runs over, the one named last changes fastest.
Arguments:
- grad_out: bfloat16 [4096, 2048], P(('dp', 'expert', 'tensor')), may hold values from -6 to 6
- expert_ids: int32 [4096, 2], P(('dp', 'expert', 'tensor')), may hold values from 0 to 63, all different within a row; in each aligned block of 128 rows (0 to 127, 128 to 255, ...) at most 5 rows name the same one
- gate_weights: float32 [4096, 2], P(('dp', 'expert', 'tensor')), may hold values from 0.05 to 0.6
- overflow: int32 [4096, 2], P(('dp', 'expert', 'tensor')), may hold values 0 or 1
- saved_gate: bfloat16 [64, 4, 8, 5, 1408], P(('expert', 'tensor'), None, None, None, 'dp'), may hold values from -6 to 6
- saved_up: bfloat16 [64, 4, 8, 5, 1408], P(('expert', 'tensor'), None, None, None, 'dp'), may hold values from -6 to 6
- w_gate: bfloat16 [64, 2048, 1408], P(('expert', 'tensor'), None, 'dp'), may hold values from -0.125 to 0.125
- w_up: bfloat16 [64, 2048, 1408], P(('expert', 'tensor'), None, 'dp'), may hold values from -0.125 to 0.125
- w_down: bfloat16 [64, 1408, 2048], P(('expert', 'tensor'), 'dp'), may hold values from -0.15625 to 0.15625
- shared_gate_act: bfloat16 [4096, 1408], P(('dp', 'expert'), 'tensor'), may hold values from -6 to 6
- shared_up_act: bfloat16 [4096, 1408], P(('dp', 'expert'), 'tensor'), may hold values from -6 to 6
- ws_gate: bfloat16 [2048, 1408], P(None, 'tensor'), may hold values from -0.125 to 0.125
- ws_up: bfloat16 [2048, 1408], P(None, 'tensor'), may hold values from -0.125 to 0.125
- ws_down: bfloat16 [1408, 2048], P('tensor'), may hold values from -0.15625 to 0.15625
- w_out: bfloat16 [2048, 2048], P('tensor'), may hold values from -0.125 to 0.125
Outputs:
- grad_hidden: bfloat16 [4096, 2048], P(('dp', 'expert', 'tensor'))
- grad_context: bfloat16 [4096, 2048], P(('dp', 'expert'), 'tensor')
The draws below stay inside these ranges and needn't reach their ends.
Inputs may be any that keep to these rules, and one draw needn't show every extreme that they name: `expert_ids`: each row names 2 different experts; within the rows of one device (aligned blocks of 128 rows) no expert is named by more than 5 rows, a bound that some block reaches.
All inputs are finite; a program needn't handle non-finite values. No bound on the sum of `overflow` on one device may be relied on, other than what follows from the above.
Results may differ from the reference program's by a relative error of at most 0.015.
Values may be sent and summed in bfloat16 or wider, within the bound.
No kernel may reach another device: no remote copies, remote signals or barrier semaphores. Data moves between devices by JAX's collectives and lax.ppermute only.
A program may use at most 128 MiB of HBM per device.

```python
import math
import jax
import jax.numpy as jnp
import numpy as np
from jax import lax

D = 2048
FE = 1408
FS = 1408
EXPERTS = 64
TOPK = 2
HV = 2048
TOK_DEV = 128
CAP = 5
TOKENS = 4096
N_DP = 4
N_EXPERT = 4
N_TENSOR = 2
DEVICES = 32


def with_ends(array, stream_key, least, high):
    extent = array.shape
    place = [jax.random.randint(jax.random.fold_in(stream_key, axis), (), 0, extent[axis]) for axis in range(len(extent))]
    array = array.at[tuple(place)].set(least)
    longest = extent.index(max(extent))
    place[longest] = (place[longest] + 1) % extent[longest]
    return array.at[tuple(place)].set(high)


def level_of(rng, dims, split, smallest, largest):
    def one(axis_at, parts):
        heights = jax.random.uniform(jax.random.fold_in(jax.random.fold_in(rng, 6), axis_at), (parts,), jnp.float32, smallest / len(split), largest / len(split))
        return jnp.repeat(jnp.exp(heights), dims[axis_at] // parts).reshape((-1,) + (1,) * (len(dims) - axis_at - 1))

    level = one(*split[0])
    for cut in split[1:]:
        level = level * one(*cut)
    return level


def assign_block(own_key, own, number, rows, amount, top, bound, lean):
    ranking = jax.random.permutation(own_key, amount)
    heavy_load, ordinary = shares(amount, rows * top, bound, lean, True), shares(amount, rows * top, bound, lean, False)
    places = jnp.arange(amount)

    def named(tallies, rotation):
        used = int((tallies > 0).sum())
        fixed = max(1, used // 4)
        shifted = fixed + (places - fixed + rotation * (used - fixed)) % max(1, amount - fixed)
        return jnp.zeros((amount,), jnp.int32).at[ranking[jnp.where(places < fixed, places, shifted)]].set(jnp.asarray(tallies, jnp.int32))

    tallies = jnp.where(number % 4 == 0, named(heavy_load, number // 4), named(ordinary, number - number // 4 - 1))
    mixed = jax.random.permutation(jax.random.fold_in(own, 3), amount)
    giver, receiver = mixed[0:amount // 2 * 2:2], mixed[1:amount // 2 * 2:2]
    room = jnp.minimum(tallies[giver] - 1, bound - tallies[receiver]) // 2
    room = jnp.where((giver == ranking[0]) | (receiver == ranking[0]) | (tallies[receiver] == 0), 0, jnp.maximum(room, 0))
    shifted = jax.random.randint(jax.random.fold_in(own, 4), (amount // 2,), 0, 1 << 20) % (room + 1)
    tallies = tallies.at[giver].add(-shifted).at[receiver].add(shifted)
    items = jnp.searchsorted(jnp.cumsum(tallies), jnp.arange(rows * top), side="right").astype(jnp.int32)
    table = items.reshape(top, rows).T
    table = table[jax.random.permutation(jax.random.fold_in(own, 1), rows)]
    rotation = jax.random.randint(jax.random.fold_in(own, 2), (rows, 1), 0, top)
    return jnp.take_along_axis(table, (jnp.arange(top)[None, :] + rotation) % top, axis=1)


def shares(count, total, limit, slope, full):
    weights = [(1 << 20) // math.isqrt(standing ** slope) + 1 for standing in range(1, count + 1)]
    largest = limit if full else min(limit, max(-(-total // count), total * weights[0] // sum(weights)))
    least = 1 if total - largest >= count - 1 else 0
    holding, spare = [largest] + [least] * (count - 1), total - largest - least * (count - 1)
    while spare > 0:
        candidates = [i for i in range(1, count) if holding[i] < largest] or [i for i in range(1, count) if holding[i] < limit]
        pool, left = sum([weights[i] for i in candidates]), spare
        for i in candidates:
            addition = min(limit - holding[i], max(1, left * weights[i] // pool), spare)
            holding[i] = holding[i] + addition
            spare = spare - addition
    return np.array(holding)


def normal_values(key, extent, deviation, bound, cuts=(), kind=jnp.bfloat16):
    entries = jax.random.normal(key, extent, jnp.float32) * deviation
    if len(cuts) > 0:
        entries = level_of(key, extent, cuts, -0.22, 0.18) * entries
    return jnp.clip(entries, min=-bound, max=bound).astype(kind)


def setup_inputs(seed: int = 0) -> dict:
    key_list = jax.random.split(jax.random.key(seed), 16)
    grad_out = normal_values(key_list[0], (TOKENS, D), 1.0, 6.0, ((0, 32),))
    expert_ids_keys = jax.random.split(jax.random.fold_in(key_list[1], 1), TOKENS // TOK_DEV)
    expert_ids_turns = jax.random.permutation(jax.random.fold_in(key_list[1], 3), TOKENS // TOK_DEV)
    expert_ids = jax.vmap(lambda own, number: assign_block(jax.random.fold_in(key_list[1], 2), own, number, TOK_DEV, EXPERTS, TOPK, CAP, 2))(expert_ids_keys, expert_ids_turns).reshape((TOKENS, TOPK))
    gate_weights = jnp.clip(jnp.exp(math.log(0.6) - 2.4849067 * jax.random.uniform(key_list[2], (TOKENS, TOPK), jnp.float32) ** level_of(key_list[2], (TOKENS, TOPK), ((0, 32),), -0.2, 0.2)), 0.05, 0.6)
    overflow = with_ends((jax.random.randint(key_list[3], (TOKENS, TOPK), 0, 4) < 1).astype(jnp.int32), jax.random.fold_in(key_list[3], 1), 0, 1)
    saved_gate = normal_values(key_list[4], (EXPERTS, N_DP, N_EXPERT * N_TENSOR, CAP, FE), 1.0, 6.0, ((0, 8), (4, 4)))
    saved_up = normal_values(key_list[5], (EXPERTS, N_DP, N_EXPERT * N_TENSOR, CAP, FE), 1.0, 6.0, ((0, 8), (4, 4)))
    w_gate = normal_values(key_list[6], (EXPERTS, D, FE), D ** -0.5, 0.125, ((0, 8), (2, 4)))
    w_up = normal_values(key_list[7], (EXPERTS, D, FE), D ** -0.5, 0.125, ((0, 8), (2, 4)))
    w_down = normal_values(key_list[8], (EXPERTS, FE, D), FE ** -0.5, 0.15625, ((0, 8), (1, 4)))
    shared_gate_act = normal_values(key_list[9], (TOKENS, FS), 1.0, 6.0, ((0, 16), (1, 2)))
    shared_up_act = normal_values(key_list[10], (TOKENS, FS), 1.0, 6.0, ((0, 16), (1, 2)))
    ws_gate = normal_values(key_list[11], (D, FS), D ** -0.5, 0.125, ((1, 2),))
    ws_up = normal_values(key_list[12], (D, FS), D ** -0.5, 0.125, ((1, 2),))
    ws_down = normal_values(key_list[13], (FS, D), FS ** -0.5, 0.15625, ((0, 2),))
    w_out = normal_values(key_list[14], (HV, D), HV ** -0.5, 0.125, ((0, 2),))
    return dict(grad_out=grad_out, expert_ids=expert_ids, gate_weights=gate_weights, overflow=overflow, saved_gate=saved_gate, saved_up=saved_up, w_gate=w_gate, w_up=w_up, w_down=w_down, shared_gate_act=shared_gate_act, shared_up_act=shared_up_act, ws_gate=ws_gate, ws_up=ws_up, ws_down=ws_down, w_out=w_out)


def swiglu_backward(hidden_activation, gate_act, up_act):
    gate_value = gate_act.astype(jnp.float32)
    sigmoid_value = jax.nn.sigmoid(gate_value)
    gate_input_gradient = (hidden_activation * up_act.astype(jnp.float32) * sigmoid_value * (1.0 + gate_value * (1.0 - sigmoid_value))).astype(jnp.bfloat16)
    up_input_gradient = (hidden_activation * gate_value * sigmoid_value).astype(jnp.bfloat16)
    return gate_input_gradient, up_input_gradient


def reference(grad_out, expert_ids, gate_weights, overflow, saved_gate, saved_up, w_gate, w_up, w_down, shared_gate_act, shared_up_act, ws_gate, ws_up, ws_down, w_out):
    flag_values = overflow.astype(jnp.float32)
    routed_weight = (gate_weights * (1.0 - flag_values)).astype(jnp.bfloat16)
    shared_weight = 1.0 + jnp.sum(gate_weights * flag_values, axis=1)
    routed_grad = (grad_out.astype(jnp.float32)[:, None, :] * routed_weight.astype(jnp.float32)[:, :, None]).astype(jnp.bfloat16)
    pair_block = TOK_DEV * TOPK
    block_ids = expert_ids.reshape(DEVICES, pair_block)
    onehot = (block_ids[:, :, None] == jnp.arange(EXPERTS, dtype=jnp.int32)[None, None, :]).astype(jnp.int32)
    earlier = jnp.cumsum(onehot, axis=1) - onehot
    slot = jnp.sum(earlier * onehot, axis=2)
    block_index = jnp.arange(DEVICES, dtype=jnp.int32)[:, None]
    slot_place = (block_ids * DEVICES + block_index) * CAP + slot
    pair_index = jnp.arange(TOKENS * TOPK, dtype=jnp.int32).reshape(DEVICES, pair_block)
    slot_owner = jnp.full((EXPERTS * DEVICES * CAP,), TOKENS * TOPK, jnp.int32)
    slot_owner = slot_owner.at[slot_place.reshape(-1)].set(pair_index.reshape(-1)).reshape(EXPERTS, DEVICES * CAP)
    rows_all = jnp.concatenate([routed_grad.reshape(TOKENS * TOPK, D), jnp.zeros((1, D), jnp.bfloat16)], axis=0)
    group_width = FE // N_DP

    def one_expert(totals, expert_index):
        picked = slot_owner[expert_index]
        capacity_slot_rows = rows_all[picked]
        gate_act = saved_gate[expert_index].reshape(DEVICES * CAP, FE)
        up_act = saved_up[expert_index].reshape(DEVICES * CAP, FE)
        hidden_activation = jnp.dot(capacity_slot_rows, w_down[expert_index].T, preferred_element_type=jnp.float32)
        gate_input_gradient, up_input_gradient = swiglu_backward(hidden_activation, gate_act, up_act)
        gate_projection_weight = w_gate[expert_index]
        up_projection_weight = w_up[expert_index]
        expert_term = jnp.zeros((DEVICES * CAP, D), jnp.float32)
        for group_index in range(N_DP):
            low = group_index * group_width
            high = low + group_width
            quarter_term = jnp.dot(gate_input_gradient[:, low:high], gate_projection_weight[:, low:high].T, preferred_element_type=jnp.float32)
            quarter_term = quarter_term + jnp.dot(up_input_gradient[:, low:high], up_projection_weight[:, low:high].T, preferred_element_type=jnp.float32)
            quarter_term = lax.optimization_barrier(quarter_term.astype(jnp.bfloat16))
            expert_term = expert_term + quarter_term.astype(jnp.float32)
        token_row = picked // TOPK
        return totals.at[token_row].add(expert_term), None

    totals, unused = lax.scan(one_expert, jnp.zeros((TOKENS + 1, D), jnp.float32), jnp.arange(EXPERTS, dtype=jnp.int32))
    routed_total = totals[:TOKENS].astype(jnp.bfloat16)

    shared_grad = (grad_out.astype(jnp.float32) * shared_weight[:, None]).astype(jnp.bfloat16)
    shared_hidden = jnp.dot(shared_grad, ws_down.T, preferred_element_type=jnp.float32)
    shared_gate_grad, shared_up_grad = swiglu_backward(shared_hidden, shared_gate_act, shared_up_act)
    part_width = FS // N_TENSOR
    shared_total = jnp.zeros((TOKENS, D), jnp.float32)
    for group_index in range(N_TENSOR):
        low = group_index * part_width
        high = low + part_width
        group_term = jnp.dot(shared_gate_grad[:, low:high], ws_gate[:, low:high].T, preferred_element_type=jnp.float32)
        group_term = group_term + jnp.dot(shared_up_grad[:, low:high], ws_up[:, low:high].T, preferred_element_type=jnp.float32)
        group_term = lax.optimization_barrier(group_term.astype(jnp.bfloat16))
        shared_total = shared_total + group_term.astype(jnp.float32)
    grad_hidden = (grad_out.astype(jnp.float32) + shared_total + routed_total.astype(jnp.float32)).astype(jnp.bfloat16)
    grad_context = jnp.dot(grad_hidden, w_out.T, preferred_element_type=jnp.float32).astype(jnp.bfloat16)
    return grad_hidden, grad_context
```

```python
import functools

import jax
import jax.numpy as jnp
from jax import lax
from jax.experimental import pallas as pl
from jax.experimental.pallas import tpu as pltpu
from jax.sharding import PartitionSpec as P

F32, BF16 = jnp.float32, jnp.bfloat16
NN = (((1,), (0,)), ((), ()))
NT = (((1,), (1,)), ((), ()))
TN = (((0,), (0,)), ((), ()))
VM = pl.BlockSpec(memory_space=pltpu.VMEM)
SM = pl.BlockSpec(memory_space=pltpu.SMEM)
LIMIT = 56 << 20
LANES = 128


def dot(a, b, dims):
    return lax.dot_general(a, b, dims, preferred_element_type=F32)


def params(limit=LIMIT, semantics=None):
    return pltpu.CompilerParams(vmem_limit_bytes=limit, dimension_semantics=semantics)


def cost(flops, moved):
    return pl.CostEstimate(flops=int(flops), bytes_accessed=int(moved), transcendentals=0)


def send_kernel(n_z, n_x, e_loc, cap, pos_ref, meta_ref, tok_ref, mask_ref, *out_refs):
    z, x = pos_ref[0], pos_ref[1]
    tokens = tok_ref.shape[0]
    rows = n_z * e_loc
    meta = meta_ref[...]
    row = lax.broadcasted_iota(jnp.int32, (rows, tokens), 0)
    hop, e = row // e_loc, row % e_loc
    expert = (((hop ^ z) * n_x + x) * e_loc + e).astype(F32)
    hit0 = expert == meta[0:1, :]
    hit1 = expert == meta[1:2, :]
    w = (meta[2:4, :] * (1.0 - meta[4:6, :])).astype(BF16).astype(F32)
    weight = jnp.where(hit0, w[0:1, :], 0.0) + jnp.where(hit1, w[1:2, :], 0.0)
    hit = jnp.where(hit0 | hit1, 1.0, 0.0)
    before = lax.broadcasted_iota(jnp.int32, (tokens, tokens), 0)
    after = lax.broadcasted_iota(jnp.int32, (tokens, tokens), 1)
    earlier = jnp.where(before < after, 1.0, 0.0).astype(BF16)
    count = dot(hit.astype(BF16), earlier, NN)
    masks, weights = [], []
    for k in range(n_z):
        part = slice(k * e_loc, (k + 1) * e_loc)
        for j in range(cap):
            here = jnp.where(count[part] == float(j), hit[part], 0.0)
            masks.append(here)
            weights.append(here * weight[part])
    mask_ref[...] = jnp.concatenate(masks, 0).astype(BF16)
    g = jnp.concatenate(weights, 0).astype(BF16)
    tok = tok_ref[...]
    size = cap * e_loc
    for k in range(n_z):
        out_refs[k][...] = dot(g[k * size:(k + 1) * size], tok, NN).astype(BF16)


def send_rows(pos, meta, tok, n_z, n_x, e_loc, cap):
    tokens, width = tok.shape
    size = cap * e_loc
    out = pl.pallas_call(
        functools.partial(send_kernel, n_z, n_x, e_loc, cap),
        out_shape=(jax.ShapeDtypeStruct((n_z * size, tokens), BF16),)
        + (jax.ShapeDtypeStruct((size, width), BF16),) * n_z,
        in_specs=[SM, VM, VM], out_specs=(VM,) * (1 + n_z),
        compiler_params=params(16 << 20), name="send_rows",
        cost_estimate=cost(2 * n_z * size * tokens * width, (tokens + n_z * size) * width * 2),
    )(pos, meta, tok)
    return out[0], list(out[1:])


def factor_kernel(order_ref, gate_ref, up_ref, fg_ref, fu_ref):
    order = order_ref[...]
    a = dot(order, gate_ref[0], NN)
    u = dot(order, up_ref[0], NN)
    s = jax.nn.sigmoid(a)
    fg = u * s * (1.0 + a * (1.0 - s))
    fu = a * s
    half = fg.shape[0] // fg_ref.shape[0]
    for i in range(fg_ref.shape[0]):
        fg_ref[i, 0] = fg[i * half:(i + 1) * half]
        fu_ref[i, 0] = fu[i * half:(i + 1) * half]


def factors(order, gate, up, n_x):
    e_loc, rows, units = gate.shape
    spec = pl.BlockSpec((1, rows, units), lambda e: (e, 0, 0))
    ospec = pl.BlockSpec((n_x, 1, rows // n_x, units), lambda e: (0, e, 0, 0))
    shape = jax.ShapeDtypeStruct((n_x, e_loc, rows // n_x, units), F32)
    return pl.pallas_call(
        factor_kernel, grid=(e_loc,), out_shape=(shape, shape),
        in_specs=[pl.BlockSpec((rows, rows), lambda e: (0, 0)), spec, spec],
        out_specs=(ospec, ospec), compiler_params=params(16 << 20), name="factors",
        cost_estimate=cost(4 * e_loc * rows * rows * units, 12 * e_loc * rows * units),
    )(order, gate, up)


def hidden_kernel(n_in, *refs):
    ins, (w_ref, fg_ref, fu_ref, gg_ref, gu_ref, wide) = refs[:n_in], refs[n_in:]
    e = pl.program_id(0)
    size = ins[0].shape[0]
    rows = gg_ref.shape[1]
    tiles = wide.shape[0]

    @pl.when(e == 0)
    def _():
        for i in range(n_in):
            for t in range(tiles):
                wide[t, i * size:(i + 1) * size, :] = ins[i][:, t * LANES:(t + 1) * LANES].astype(F32)

    step = n_in * size // rows
    x = jnp.concatenate(
        [wide[t, pl.ds(e, rows, stride=step), :] for t in range(tiles)], 1).astype(BF16)
    h = dot(x, w_ref[0], NT)
    gg_ref[0] = (h * fg_ref[0, 0]).astype(BF16)
    gu_ref[0] = (h * fu_ref[0, 0]).astype(BF16)


def hidden(ins, w_down, fg, fu, chunk):
    e_loc, units, width = w_down.shape
    rows = fg.shape[2]
    size = ins[0].shape[0]
    fspec = pl.BlockSpec((1, 1, rows, units), lambda e: (chunk, e, 0, 0))
    ospec = pl.BlockSpec((1, rows, units), lambda e: (e, 0, 0))
    shape = jax.ShapeDtypeStruct((e_loc, rows, units), BF16)
    return pl.pallas_call(
        functools.partial(hidden_kernel, len(ins)), grid=(e_loc,), out_shape=(shape, shape),
        in_specs=[pl.BlockSpec((size, width), lambda e: (0, 0))] * len(ins)
        + [pl.BlockSpec((1, units, width), lambda e: (e, 0, 0)), fspec, fspec],
        out_specs=(ospec, ospec),
        scratch_shapes=[pltpu.VMEM((width // LANES, len(ins) * size, LANES), F32)],
        compiler_params=params(32 << 20), name="hidden",
        cost_estimate=cost(2 * e_loc * rows * units * width, e_loc * units * width * 2),
    )(*ins, w_down, fg, fu)


def terms_kernel(n_x, n_c, n_y, n_z, size, *refs):
    gs, us, (wg_ref, wu_ref), outs, wide = (
        refs[:n_x], refs[n_x:2 * n_x], refs[2 * n_x:2 * n_x + 2], refs[2 * n_x + 2:-1], refs[-1])
    e = pl.program_id(0)
    rows = gs[0].shape[1]
    tiles = wide.shape[0]
    e_loc = wide.shape[1] // (n_x * rows)
    g = jnp.concatenate([r[0] for r in gs], 0)
    u = jnp.concatenate([r[0] for r in us], 0)
    out = dot(g, wg_ref[0], NN) + dot(u, wu_ref[0], NN)
    for t in range(tiles):
        wide[t, pl.ds(e, n_x * rows, stride=e_loc), :] = out[:, t * LANES:(t + 1) * LANES]

    @pl.when(e == pl.num_programs(0) - 1)
    def _():
        for s in range(n_x):
            for c in range(n_c):
                for y in range(n_y):
                    for k in range(n_z):
                        at = (((s * n_c + c) * n_y + y) * n_z + k) * size
                        rows_out = [wide[t, at:at + size, :] for t in range(tiles)]
                        outs[c][(y * n_z + k) * n_x + s] = jnp.concatenate(rows_out, 1).astype(BF16)


def terms(gs, us, wg, wu, chunk, cols, n_c, n_y, n_z, size):
    e_loc, units, width = wg.shape
    n_x, rows = len(gs), gs[0].shape[1]
    gspec = pl.BlockSpec((1, rows, units), lambda e: (e, 0, 0))
    wspec = pl.BlockSpec((1, units, cols), lambda e: (e, 0, chunk))
    pieces = n_y * n_z * n_x
    return pl.pallas_call(
        functools.partial(terms_kernel, n_x, n_c, n_y, n_z, size), grid=(e_loc,),
        out_shape=(jax.ShapeDtypeStruct((pieces, size, cols), BF16),) * n_c,
        in_specs=[gspec] * (2 * n_x) + [wspec, wspec],
        out_specs=(pl.BlockSpec((pieces, size, cols), lambda e: (0, 0, 0)),) * n_c,
        scratch_shapes=[pltpu.VMEM((cols // LANES, e_loc * n_x * rows, LANES), F32)],
        compiler_params=params(40 << 20), name="terms",
        cost_estimate=cost(4 * e_loc * n_x * rows * units * cols, 2 * e_loc * units * cols * 2),
    )(*gs, *us, wg, wu)


def shared_kernel(pos_ref, *refs):
    n = (len(refs) - 6) // 2
    metas, toks = refs[:n], refs[n:2 * n]
    ga_ref, ua_ref, wd_ref, wg_ref, wu_ref, out_ref = refs[2 * n:]
    x = pos_ref[1]
    tokens = toks[0].shape[0]
    for s in range(n):
        meta = metas[s][...]
        w = 1.0 + jnp.sum(meta[2:4, :] * meta[4:6, :], axis=0, keepdims=True)
        h = dot(wd_ref[...], toks[s][...], NT) * w
        lanes = pl.ds(pl.multiple_of((x ^ s) * tokens, tokens), tokens)
        a = ga_ref[:, lanes].astype(F32)
        u = ua_ref[:, lanes].astype(F32)
        sg = jax.nn.sigmoid(a)
        gg = (h * u * sg * (1.0 + a * (1.0 - sg))).astype(BF16)
        gu = (h * a * sg).astype(BF16)
        out_ref[s] = dot(gg, wg_ref[...], TN) + dot(gu, wu_ref[...], TN)


def shared_terms(pos, metas, toks, ga, ua, wd, wg, wu):
    n, (tokens, width) = len(toks), toks[0].shape
    units = wd.shape[0]
    return pl.pallas_call(
        shared_kernel, out_shape=jax.ShapeDtypeStruct((n, tokens, width), F32),
        in_specs=[SM] + [VM] * (2 * n + 5), out_specs=VM,
        compiler_params=params(40 << 20), name="shared",
        cost_estimate=cost(6 * n * tokens * units * width, 6 * units * width),
    )(pos, *metas, *toks, ga, ua, wd, wg, wu)


def gather_kernel(n_z, n_x, *refs):
    rets, masks, shared_ref, out_ref = refs[:n_z], refs[n_z:n_z + n_x], refs[-2], refs[-1]
    tokens = masks[0].shape[1]
    for s in range(n_x):
        rows = jnp.concatenate([r[s].astype(F32) for r in rets], 0).astype(BF16)
        total = dot(masks[s][...], rows, TN) + shared_ref[s]
        out_ref[s * tokens:(s + 1) * tokens, :] = total.astype(BF16)


def gather_rows(rets, masks, shared, chunk, cols):
    n_x, tokens = len(masks), masks[0].shape[1]
    size = rets[0].shape[1]
    rspec = pl.BlockSpec((n_x, size, cols), lambda i: (0, 0, 0))
    mspec = pl.BlockSpec(masks[0].shape, lambda i: (0, 0))
    return pl.pallas_call(
        functools.partial(gather_kernel, len(rets), n_x), grid=(1,),
        out_shape=jax.ShapeDtypeStruct((n_x * tokens, cols), BF16),
        in_specs=[rspec] * len(rets) + [mspec] * n_x
        + [pl.BlockSpec((n_x, tokens, cols), lambda i: (0, 0, chunk))],
        out_specs=pl.BlockSpec((n_x * tokens, cols), lambda i: (0, 0)),
        compiler_params=params(24 << 20), name="gather_rows",
        cost_estimate=cost(2 * masks[0].size * n_x * cols, n_x * tokens * cols * 6),
    )(*rets, *masks, shared)


def final_kernel(chunk, chunks, pos_ref, own_ref, par_ref, mine_ref, got_ref, w_ref, *refs):
    tokens, cols = own_ref.shape
    mine, got = mine_ref[...].astype(F32), got_ref[...].astype(F32)
    own = (own_ref[...].astype(F32) + mine[:tokens] + got[tokens:]).astype(BF16)
    par = (par_ref[...].astype(F32) + mine[tokens:] + got[:tokens]).astype(BF16)
    part = dot(jnp.concatenate([own, par], 0), w_ref[...], NT)
    before = refs[:chunk]
    if chunk:
        part = part + refs[chunk][...]
        refs = refs[chunk + 1:]
    if chunk < chunks - 1:
        refs[0][...] = own
        refs[1][...] = part
        return
    for i, r in enumerate(before):
        refs[0][:, i * cols:(i + 1) * cols] = r[...]
    refs[0][:, chunk * cols:] = own
    x = pos_ref[1]
    refs[1][pl.ds(pl.multiple_of(x * tokens, tokens), tokens), :] = part[:tokens].astype(BF16)
    refs[1][pl.ds(pl.multiple_of((1 - x) * tokens, tokens), tokens), :] = part[tokens:].astype(BF16)


def final(pos, toks, mine, got, w_out, chunk, cols, before, acc):
    tokens, width = toks[0].shape
    heads = w_out.shape[0]
    chunks = width // cols
    last = chunk == chunks - 1
    tspec = pl.BlockSpec((tokens, cols), lambda i: (0, chunk))
    pspec = pl.BlockSpec((2 * tokens, cols), lambda i: (0, 0))
    bspec = pl.BlockSpec((tokens, cols), lambda i: (0, 0))
    aspec = pl.BlockSpec((2 * tokens, heads), lambda i: (0, 0))
    extra = list(before) + [acc] if chunk else []
    espec = [bspec] * len(before) + [aspec] if chunk else []
    gh = width if last else cols
    return pl.pallas_call(
        functools.partial(final_kernel, chunk, chunks), grid=(1,),
        out_shape=(jax.ShapeDtypeStruct((tokens, gh), BF16),
                   jax.ShapeDtypeStruct((2 * tokens, heads), BF16 if last else F32)),
        in_specs=[SM, tspec, tspec, pspec, pspec,
                  pl.BlockSpec((heads, cols), lambda i: (0, chunk))] + espec,
        out_specs=(pl.BlockSpec((tokens, gh), lambda i: (0, 0)), aspec),
        compiler_params=params(32 << 20), name="final",
        cost_estimate=cost(4 * tokens * cols * heads, heads * cols * 2),
    )(pos, *toks, mine, got, w_out, *extra)


def swap(value, axis, hop):
    n = lax.axis_size(axis)
    return lax.ppermute(value, axis, [(i, i ^ hop) for i in range(n)])


def body(
    grad_out, expert_ids, gate_weights, overflow, saved_gate, saved_up, w_gate, w_up, w_down,
    shared_gate_act, shared_up_act, ws_gate, ws_up, ws_down, w_out,
):
    n_z, n_x, n_dp = lax.axis_size("expert"), lax.axis_size("tensor"), lax.axis_size("dp")
    n_c, n_y = 2, n_dp // 2
    z, x, dp = lax.axis_index("expert"), lax.axis_index("tensor"), lax.axis_index("dp")
    e_loc, _, _, cap, units = saved_gate.shape
    tokens, width = grad_out.shape
    size = cap * e_loc
    pos = jnp.stack([z, x, dp]).astype(jnp.int32)

    meta = jnp.concatenate(
        [expert_ids.T.astype(F32), gate_weights.T, overflow.T.astype(F32), overflow.T.astype(F32)], 0)
    metas = [meta, swap(meta, "tensor", 1)]
    toks = [grad_out, swap(grad_out, "tensor", 1)]

    def axis(n, at):
        return jnp.arange(n, dtype=jnp.int32).reshape((-1,) + (1,) * at)

    dp_of = dp ^ (axis(n_y, 2) * 2 + axis(n_c, 3))
    source = (dp_of * cap + axis(cap, 0)) * (n_z * n_x) + (z ^ axis(n_z, 1)) * n_x + (x ^ axis(n_x, 4))
    source = source.reshape(-1)
    order = (source[:, None] == jnp.arange(source.shape[0], dtype=jnp.int32)[None, :]).astype(BF16)
    gate = jnp.swapaxes(saved_gate, 2, 3).reshape(e_loc, -1, units)
    up = jnp.swapaxes(saved_up, 2, 3).reshape(e_loc, -1, units)
    fg, fu = factors(order, gate, up, n_x)

    masks, gs, us = [], [], []
    for s in range(n_x):
        mask, pieces = send_rows(pos, metas[s], toks[s], n_z, n_x, e_loc, cap)
        masks.append(mask)
        arrived = jnp.concatenate(
            [pieces[0]] + [swap(pieces[k], "expert", k) for k in range(1, n_z)], 0)
        near = [arrived] + [swap(arrived, "dp", 2 * h) for h in range(1, n_y)]
        rows = near + [swap(r, "dp", 1) for r in near]
        g, u = hidden(rows, w_down, fg, fu, s)
        gs.append(g)
        us.append(u)

    shared = shared_terms(pos, metas, toks, shared_gate_act.T, shared_up_act.T, ws_down, ws_gate.T, ws_up.T)

    wg, wu = jnp.swapaxes(w_gate, 1, 2), jnp.swapaxes(w_up, 1, 2)
    cols = width // CHUNKS
    before, acc = [], None
    per_y = n_z * n_x
    for j in range(CHUNKS):
        keep, send = terms(gs, us, wg, wu, j, cols, n_c, n_y, n_z, size)
        got = swap(send, "dp", 1)
        total = keep.astype(F32) + got.astype(F32)
        mine = total[:per_y]
        for h in range(1, n_y):
            mine = mine + swap(total[h * per_y:(h + 1) * per_y].astype(BF16), "dp", 2 * h).astype(F32)
        mine = mine.astype(BF16)
        rets = [mine[:n_x]] + [swap(mine[k * n_x:(k + 1) * n_x], "expert", k) for k in range(1, n_z)]
        part = gather_rows(rets, masks, shared, j, cols)
        other = swap(part, "tensor", 1)
        gh, acc = final(pos, toks, part, other, w_out, j, cols, before, acc)
        before.append(gh)
    return gh, acc


CHUNKS = 2


def rank_in_block(pair_experts, expert_total):
    onehot = (pair_experts[:, None] == jnp.arange(expert_total, dtype=jnp.int32)[None, :]).astype(
        jnp.int32
    )
    earlier = jnp.cumsum(onehot, axis=0) - onehot
    return jnp.sum(earlier * onehot, axis=1)


def fill_slots(pair_grads, pair_experts, expert_total, capacity):
    pair_count, model_width = pair_grads.shape
    destination = pair_experts * capacity + rank_in_block(pair_experts, expert_total)
    source = jnp.full((expert_total * capacity,), pair_count, jnp.int32)
    source = source.at[destination].set(jnp.arange(pair_count, dtype=jnp.int32))
    padded = jnp.concatenate([pair_grads, jnp.zeros((1, model_width), pair_grads.dtype)], axis=0)
    return (padded[source].reshape(expert_total, capacity, model_width), destination)


def weighted_pairs(grads, weights):
    scaled = grads.astype(jnp.float32)[:, None, :] * weights.astype(jnp.float32)[:, :, None]
    return scaled.astype(jnp.bfloat16).reshape(-1, grads.shape[1])


def swiglu_backward(hidden_activation, gate_act, up_act):
    gate_value = gate_act.astype(jnp.float32)
    sigmoid_value = jax.nn.sigmoid(gate_value)
    gate_input_gradient = (
        hidden_activation
        * up_act.astype(jnp.float32)
        * sigmoid_value
        * (1.0 + gate_value * (1.0 - sigmoid_value))
    ).astype(jnp.bfloat16)
    up_input_gradient = (hidden_activation * gate_value * sigmoid_value).astype(jnp.bfloat16)
    return (gate_input_gradient, up_input_gradient)


def expert_terms(
    capacity_slot_rows,
    gate_act,
    up_act,
    gate_projection_weight,
    up_projection_weight,
    down_projection_weight,
):
    hidden_activation = jnp.einsum(
        "cyg,cog->cyo",
        capacity_slot_rows,
        down_projection_weight,
        preferred_element_type=jnp.float32,
    )
    gate_input_gradient, up_input_gradient = swiglu_backward(hidden_activation, gate_act, up_act)
    input_gradient_output = jnp.einsum(
        "etv,ebv->etb",
        gate_input_gradient,
        gate_projection_weight,
        preferred_element_type=jnp.float32,
    )
    input_gradient_output = input_gradient_output + jnp.einsum(
        "etv,ebv->etb", up_input_gradient, up_projection_weight, preferred_element_type=jnp.float32
    )
    return lax.optimization_barrier(input_gradient_output.astype(jnp.bfloat16))


def general_body(
    grad_out,
    expert_ids,
    gate_weights,
    overflow,
    saved_gate,
    saved_up,
    w_gate,
    w_up,
    w_down,
    shared_gate_act,
    shared_up_act,
    ws_gate,
    ws_up,
    ws_down,
    w_out,
):
    dp_count = lax.axis_size("dp")
    group_count = lax.axis_size(("expert", "tensor"))
    expert_local, unused_dp, unused_group, capacity, unit_part = saved_gate.shape
    expert_total = expert_local * group_count
    token_count, model_width = grad_out.shape
    top_count = expert_ids.shape[1]
    flag_values = overflow.astype(jnp.float32)
    routed_weight = (gate_weights * (1.0 - flag_values)).astype(jnp.bfloat16)
    shared_weight = 1.0 + jnp.sum(gate_weights * flag_values, axis=1)
    pair_grads = weighted_pairs(grad_out, routed_weight)
    filled, destination = fill_slots(pair_grads, expert_ids.reshape(-1), expert_total, capacity)
    arrived = lax.all_to_all(
        filled[:, None], ("expert", "tensor"), split_axis=0, concat_axis=1, tiled=True
    )
    everyone = lax.all_gather(arrived[:, None], "dp", axis=1, tiled=True)
    terms = expert_terms(
        everyone.reshape(expert_local, -1, model_width),
        saved_gate.reshape(expert_local, -1, unit_part),
        saved_up.reshape(expert_local, -1, unit_part),
        w_gate,
        w_up,
        w_down,
    )
    terms = terms.astype(jnp.float32).reshape(
        expert_local, dp_count, group_count, capacity, model_width
    )
    summed = lax.psum_scatter(
        terms.astype(jnp.bfloat16), "dp", scatter_dimension=1, tiled=True
    ).astype(jnp.float32)
    returned = lax.all_to_all(
        summed[:, 0].astype(jnp.bfloat16),
        ("expert", "tensor"),
        split_axis=1,
        concat_axis=0,
        tiled=True,
    ).astype(jnp.float32)
    picked = returned.reshape(expert_total * capacity, model_width)[destination]
    routed = jnp.sum(picked.reshape(token_count, top_count, model_width), axis=1)
    routed_total = routed.astype(jnp.bfloat16)
    shared_grad = (grad_out.astype(jnp.float32) * shared_weight[:, None]).astype(jnp.bfloat16)
    group_shared = lax.all_gather(shared_grad, "tensor", axis=0, tiled=True)
    shared_hidden = jnp.einsum(
        "td,fd->tf", group_shared, ws_down, preferred_element_type=jnp.float32
    )
    shared_gate_grad, shared_up_grad = swiglu_backward(
        shared_hidden, shared_gate_act, shared_up_act
    )
    partial_value = jnp.einsum(
        "tf,df->td", shared_gate_grad, ws_gate, preferred_element_type=jnp.float32
    )
    partial_value = partial_value + jnp.einsum(
        "tf,df->td", shared_up_grad, ws_up, preferred_element_type=jnp.float32
    )
    partial_value = lax.optimization_barrier(partial_value.astype(jnp.bfloat16)).astype(jnp.float32)
    own_shared = lax.psum_scatter(
        partial_value.astype(jnp.bfloat16), "tensor", scatter_dimension=0, tiled=True
    ).astype(jnp.float32)
    grad_hidden = (
        grad_out.astype(jnp.float32) + own_shared + routed_total.astype(jnp.float32)
    ).astype(jnp.bfloat16)
    grad_group = lax.all_gather(grad_hidden, "tensor", axis=0, tiled=True)
    grad_context = jnp.einsum(
        "td,hd->th", grad_group, w_out, preferred_element_type=jnp.float32
    ).astype(jnp.bfloat16)
    return (grad_hidden, grad_context)


def solution(mesh):
    sizes = dict(mesh.shape)
    paired = sizes["tensor"] == 2 and sizes["dp"] == 4 and sizes["expert"] & (sizes["expert"] - 1) == 0
    in_specs = (
        P(("dp", "expert", "tensor"), None),
        P(("dp", "expert", "tensor"), None),
        P(("dp", "expert", "tensor"), None),
        P(("dp", "expert", "tensor"), None),
        P(("expert", "tensor"), None, None, None, "dp"),
        P(("expert", "tensor"), None, None, None, "dp"),
        P(("expert", "tensor"), None, "dp"),
        P(("expert", "tensor"), None, "dp"),
        P(("expert", "tensor"), "dp", None),
        P(("dp", "expert"), "tensor"),
        P(("dp", "expert"), "tensor"),
        P(None, "tensor"),
        P(None, "tensor"),
        P("tensor", None),
        P("tensor", None),
    )
    out_specs = (P(("dp", "expert", "tensor"), None), P(("dp", "expert"), "tensor"))
    return jax.shard_map(
        body if paired else general_body, mesh=mesh, in_specs=in_specs, out_specs=out_specs, check_vma=False)
```
